128 devices in a mesh: grid: 8 (over x, core), proc: 16 (over z, y).
Axes of the slice: x: 4, y: 4, z: 4, core: 2. Of those that a mesh axis runs over, the one named last changes fastest.
Arguments:
- rhs: float32 [3, 8, 16, 256, 1024], P(None, 'grid', 'proc'), may hold values from -6 to 6
- tile_pairs: int32 [2, 8, 16, 32], P(None, 'grid', 'proc'), may hold values from -1 to 31, as said below
- tiles: bfloat16 [2, 8, 16, 32, 256, 256], P(None, 'grid', 'proc'), may hold values from -0.09375 to 0.09375
- dinv: float32 [3, 8, 16, 256, 256], P(None, 'grid', 'proc'), as said below
Outputs:
- solution: float32 [3, 8, 16, 256, 1024], P(None, 'grid', 'proc')
The draws below stay inside these ranges and needn't reach their ends.
Inputs may be any that keep to these rules, and one draw needn't show every extreme that they name: tile_pairs[t, g, p] holds distinct pair numbers in its first slots and -1 in the others; pair number q names block column q mod 16 and destination q // 16 (0: the same grid, 1: the partner grid). In every transition and grid one device uses all 32 slots and the others use 2 to 16 of them. Each dinv tile is lower triangular with diagonal entries between 0.5 and 1.4.
All inputs are finite; a program needn't handle non-finite values.
Results may differ from the reference program's by a relative error of at most 0.0021.
Values may be sent and summed in bfloat16 or wider, within the bound.
No kernel may reach another device: no remote copies, remote signals or barrier semaphores. Data moves between devices by JAX's collectives and lax.ppermute only.
A program may use at most 128 MiB of HBM per device.

```python
import math
import jax
import jax.numpy as jnp
import numpy as np
from jax import lax

TILE = 256
RHS = 1024
LEVELS = 3
GRIDS = 8
PROCS = 16
CAP = 32
TRANS = 2


def draw_tile_pairs(key, part):
    row_total = TRANS * GRIDS * PROCS
    key_list = jax.random.split(jax.random.fold_in(key, 11), row_total)
    orders = jax.vmap(lambda single: jax.random.permutation(single, CAP))(key_list)
    orders = orders.reshape(TRANS, GRIDS, PROCS, CAP).astype(jnp.int32)
    counts = jax.random.randint(jax.random.fold_in(key, 12), (TRANS, GRIDS, PROCS), 2, CAP // 2 + 1)
    fullest = jax.random.randint(jax.random.fold_in(key, 13), (TRANS, GRIDS, 1), 0, PROCS)
    device_rank = lax.broadcasted_iota(jnp.int32, (TRANS, GRIDS, PROCS), 2)
    counts = jnp.where(device_rank == fullest, CAP, counts)
    slot_index = lax.broadcasted_iota(jnp.int32, (TRANS, GRIDS, PROCS, CAP), 3)
    return jnp.where(slot_index < counts[..., None], orders, -1).astype(jnp.int32)


def draw_dinv(key, part):
    first_key = jax.random.fold_in(key, 21)
    second_key = jax.random.fold_in(key, 22)
    full_shape = (LEVELS, GRIDS, PROCS, TILE, TILE)
    row_ids = lax.broadcasted_iota(jnp.int32, (TILE, TILE), 0)
    col_ids = lax.broadcasted_iota(jnp.int32, (TILE, TILE), 1)
    lower_mask = (row_ids > col_ids).astype(jnp.float32)
    diagonal_mask = (row_ids == col_ids).astype(jnp.float32)
    off_part = jax.random.normal(first_key, full_shape, jnp.float32) * (0.5 / math.sqrt(TILE))
    diag_part = jax.random.uniform(second_key, full_shape[:-1], jnp.float32, 0.6, 1.2)
    return off_part * lower_mask + diagonal_mask * diag_part[..., None]


def block_levels(stream_key, shape, cuts, smallest, high):
    def one(dim, parts):
        steps = jax.random.uniform(jax.random.fold_in(jax.random.fold_in(stream_key, 6), dim), (parts,), jnp.float32, smallest / len(cuts), high / len(cuts))
        return jnp.repeat(jnp.exp(steps), shape[dim] // parts).reshape((-1,) + (1,) * (len(shape) - dim - 1))

    gain = one(*cuts[0])
    for cut in cuts[1:]:
        gain = gain * one(*cut)
    return gain


def noise(key, extent, spread, reach, pieces=(), kind=jnp.bfloat16):
    result = spread * jax.random.normal(key, extent, jnp.float32)
    if pieces:
        result = result * block_levels(key, extent, pieces, -0.22, 0.18)
    return jnp.clip(result, -reach, reach).astype(kind)


def setup_inputs(seed: int = 0) -> dict:
    splits = jax.random.split(jax.random.key(seed), 5)
    return {
        "rhs": noise(splits[0], (LEVELS, GRIDS, PROCS, TILE, RHS), 1.0, 6.0, ((1, 8), (2, 16)), jnp.float32),
        "tile_pairs": draw_tile_pairs(jax.random.fold_in(splits[4], 71), 0),
        "tiles": noise(splits[2], (TRANS, GRIDS, PROCS, CAP, TILE, TILE), (TILE * PROCS) ** -0.5, 0.09375, ((1, 8), (2, 16))),
        "dinv": draw_dinv(jax.random.fold_in(splits[4], 71), 0),
    }


def device_sums(device_inputs, rounded):
    pairs, tile_set, grid_index = device_inputs
    labels = lax.broadcasted_iota(jnp.int32, (CAP, CAP), 1)
    onehot = (pairs[:, None] == labels).astype(jnp.float32)
    dense = jnp.einsum("sq,sij->qij", onehot, tile_set.astype(jnp.float32), precision=lax.Precision.HIGHEST)
    dense = dense.reshape(2, PROCS, TILE, TILE)
    blocks = lax.dynamic_index_in_dim(rounded, grid_index, 0, keepdims=False).astype(jnp.float32)
    return jnp.einsum("dkij,kjr->dir", dense, blocks, precision=lax.Precision.HIGHEST)


def solve_blocks(factors, values):
    return jnp.einsum("gpij,gpjr->gpir", factors, values, precision=lax.Precision.HIGHEST)


def reference(rhs, tile_pairs, tiles, dinv):
    current = solve_blocks(dinv[0], rhs[0])
    solved = [current]
    owners = (jnp.arange(GRIDS * PROCS, dtype=jnp.int32) // PROCS).astype(jnp.int32)
    for height in range(1, LEVELS):
        rounded = current.astype(jnp.bfloat16)
        inputs = (tile_pairs[height - 1].reshape(GRIDS * PROCS, CAP),
                  tiles[height - 1].reshape(GRIDS * PROCS, CAP, TILE, TILE),
                  owners)
        partial_value = lax.map(lambda device_inputs: device_sums(device_inputs, rounded), inputs)
        partial_value = partial_value.reshape(GRIDS, PROCS, 2, TILE, RHS)
        partner_rows = np.arange(GRIDS) ^ (1 << (height - 1))
        update = partial_value[:, :, 0] + partial_value[partner_rows, :, 1]
        current = solve_blocks(dinv[height], rhs[height] - update)
        solved.append(current)
    return jnp.stack(solved)
```

```python
import jax
import jax.numpy as jnp
import numpy as np
from jax import lax
from jax.experimental import pallas as pl
from jax.experimental.pallas import tpu as pltpu
from jax.sharding import PartitionSpec as P

AXES = ("grid", "proc")
SIDE = 4
CHUNKS = (("y", 0, 256), ("z", 256, 256), ("y", 512, 256), ("z", 768, 256))


def ring_partner(place, flip):
    odd = place % 2
    return (place + 1 - 2 * (odd ^ flip)) % SIDE


def exchange_route(shape, axis, step):
    grids, procs = shape
    route = []
    for g in range(grids):
        for p in range(procs):
            z, y = divmod(p, SIDE)
            flip = (g + step) % 2
            if axis == "y":
                y = ring_partner(y, flip)
            else:
                z = ring_partner(z, flip)
            route.append((g * procs + p, g * procs + z * SIDE + y))
    return route


def gather_order(first, shape):
    grids, procs = shape
    table = np.zeros((grids, procs, procs), np.int32)
    for g in range(grids):
        for p in range(procs):
            z, y = divmod(p, SIDE)
            flip = g % 2

            def seq(t):
                near, far = ring_partner(t, flip), ring_partner(t, 1 - flip)
                return [t, near, far, ring_partner(far, flip)]

            ys, zs = seq(y), seq(z)
            if first == "y":
                held = [a * SIDE + b for a in zs for b in ys]
            else:
                held = [a * SIDE + b for b in ys for a in zs]
            table[g, p] = held
    return table


def gather_blocks(block, first, shape):
    held = block[None]
    for axis in (first, "z" if first == "y" else "y"):
        for step in (0, 1):
            got = lax.ppermute(held, AXES, exchange_route(shape, axis, step))
            held = jnp.concatenate([held, got])
    return held


def from_partner(block, apart, shape):
    grids, procs = shape
    route = [
        (g * procs + p, (g ^ (1 << apart)) * procs + p) for g in range(grids) for p in range(procs)
    ]
    return lax.ppermute(block, AXES, route)


def table_kernel(where_ref, count_ref, tiles_ref, *refs):
    *out_refs, held, sem = refs
    count = count_ref[0]

    def copy(s):
        return pltpu.make_async_copy(tiles_ref.at[s], held.at[s], sem)

    def start(s, c):
        copy(s).start()
        return c

    def wait(s, c):
        copy(s).wait()
        return c

    lax.fori_loop(0, count, start, 0)
    lax.fori_loop(0, count, wait, 0)
    size = held.shape[1]
    for kind, out_ref in enumerate(out_refs):
        pairs = where_ref.shape[1]
        for q in range(pairs):
            d, k = divmod(q, pairs // 2)
            rows, cols = pl.ds(d * size, size), pl.ds(k * size, size)
            slot = where_ref[kind, q]

            @pl.when(slot >= 0)
            def _():
                out_ref[rows, cols] = held[jnp.maximum(slot, 0)]

            @pl.when(slot < 0)
            def _():
                out_ref[rows, cols] = jnp.zeros((size, size), out_ref.dtype)


def build_tables(where, count, tiles):
    slots, size, _ = tiles.shape
    kinds = where.shape[0]
    out = jax.ShapeDtypeStruct((2 * size, slots // 2 * size), tiles.dtype)
    return pl.pallas_call(
        table_kernel,
        out_shape=[out] * kinds,
        in_specs=[
            pl.BlockSpec(memory_space=pltpu.SMEM),
            pl.BlockSpec(memory_space=pltpu.SMEM),
            pl.BlockSpec(memory_space=pl.ANY),
        ],
        out_specs=[pl.BlockSpec(memory_space=pltpu.VMEM)] * kinds,
        scratch_shapes=[pltpu.VMEM(tiles.shape, tiles.dtype), pltpu.SemaphoreType.DMA],
        compiler_params=pltpu.CompilerParams(vmem_limit_bytes=24 << 20),
        cost_estimate=pl.CostEstimate(flops=0, bytes_accessed=12 << 20, transcendentals=0),
    )(where, count, tiles)


def diagonal_solve(factor, values):
    return jnp.dot(
        factor, values, precision=lax.Precision.HIGH, preferred_element_type=jnp.float32
    )


def make_body(shape):
    orders = {first: gather_order(first, shape) for first in ("y", "z")}

    def body(rhs, tile_pairs, tiles, dinv):
        levels, size = rhs.shape[0], rhs.shape[3]
        rhs, dinv, tiles, pairs = rhs[:, 0, 0], dinv[:, 0, 0], tiles[:, 0, 0], tile_pairs[:, 0, 0]
        slots = pairs.shape[1]
        me = lax.axis_index("grid") * shape[1] + lax.axis_index("proc")
        held = jnp.stack([jnp.asarray(orders[f].reshape(-1, shape[1]))[me] for f in ("y", "z")])
        wanted = jnp.concatenate([held, held + shape[1]], 1)
        hit = pairs[:, None, None, :] == wanted[None, :, :, None]
        index = lax.broadcasted_iota(jnp.int32, hit.shape, 3)
        where = jnp.max(jnp.where(hit, index, -1), -1)
        counts = jnp.sum((pairs >= 0).astype(jnp.int32), 1)
        tables = [
            dict(zip(("y", "z"), build_tables(where[t], counts[t : t + 1], tiles[t])))
            for t in range(levels - 1)
        ]
        solved = [[None] * len(CHUNKS) for _ in range(levels)]
        for c, (first, start, width) in enumerate(CHUNKS):
            solved[0][c] = diagonal_solve(dinv[0], rhs[0, :, start : start + width])
        for level in range(1, levels):
            for c, (first, start, width) in enumerate(CHUNKS):
                outgoing = solved[level - 1][c].astype(jnp.bfloat16)
                blocks = gather_blocks(outgoing, first, shape)
                partial = jnp.dot(
                    tables[level - 1][first],
                    blocks.reshape(-1, width),
                    preferred_element_type=jnp.float32,
                )
                update = partial[:size] + from_partner(partial[size:], level - 1, shape)
                solved[level][c] = diagonal_solve(
                    dinv[level], rhs[level, :, start : start + width] - update
                )
        out = jnp.stack([jnp.concatenate(row, 1) for row in solved])
        return out[:, None, None]

    return body


def solution(mesh):
    shape = (mesh.shape["grid"], mesh.shape["proc"])
    return jax.shard_map(
        make_body(shape),
        mesh=mesh,
        in_specs=(
            P(None, "grid", "proc", None, None),
            P(None, "grid", "proc", None),
            P(None, "grid", "proc", None, None, None),
            P(None, "grid", "proc", None, None),
        ),
        out_specs=P(None, "grid", "proc", None, None),
        check_vma=False,
    )
```

```python
import jax
import jax.numpy as jnp
import numpy as np
from jax import lax
from jax.experimental import pallas as pl
from jax.experimental.pallas import tpu as pltpu
from jax.sharding import PartitionSpec as P

AXES = ("grid", "proc")
SIDE = 4
VM = 24
LINK = jnp.bfloat16
CHUNKS = (("y", 0, 256), ("z", 256, 256), ("y", 512, 256), ("z", 768, 256))


def ring_partner(place, flip):
    odd = place % 2
    return (place + 1 - 2 * (odd ^ flip)) % SIDE


def exchange_route(shape, axis, step):
    grids, procs = shape
    route = []
    for g in range(grids):
        for p in range(procs):
            z, y = divmod(p, SIDE)
            flip = (g + step) % 2
            if axis == "y":
                y = ring_partner(y, flip)
            else:
                z = ring_partner(z, flip)
            route.append((g * procs + p, g * procs + z * SIDE + y))
    return route


def gather_order(first, shape):
    grids, procs = shape
    table = np.zeros((grids * procs, procs), np.int32)
    for g in range(grids):
        for p in range(procs):

            def seq(t, flip=g % 2):
                near, far = ring_partner(t, flip), ring_partner(t, 1 - flip)
                return [t, near, far, ring_partner(far, flip)]

            z, y = divmod(p, SIDE)
            zs, ys = seq(z), seq(y)
            if first == "y":
                held = [a * SIDE + b for a in zs for b in ys]
            else:
                held = [a * SIDE + b for b in ys for a in zs]
            table[g * procs + p] = held
    return table


def gather_blocks(block, first, shape):
    held = block[None]
    for axis in (first, "z" if first == "y" else "y"):
        for step in (0, 1):
            got = lax.ppermute(held, AXES, exchange_route(shape, axis, step))
            held = jnp.concatenate([held, got])
    return held.reshape(-1, held.shape[-1])


def from_partner(block, shape, level):
    grids, procs = shape
    apart = 1 << level
    route = [(g * procs + p, (g ^ apart) * procs + p) for g in range(grids) for p in range(procs)]
    return lax.ppermute(block, AXES, route)


def table_kernel(level, where_ref, count_ref, tiles_ref, *refs):
    *out_refs, held, sem = refs
    count = count_ref[level]

    def copy(s):
        return pltpu.make_async_copy(tiles_ref.at[level, 0, 0, s], held.at[s], sem)

    def start(s, c):
        copy(s).start()
        return c

    def wait(s, c):
        copy(s).wait()
        return c

    lax.fori_loop(0, count, start, 0)
    lax.fori_loop(0, count, wait, 0)
    size = held.shape[1]
    for n, out_ref in enumerate(out_refs):
        kind, d = divmod(n, 2)
        blocks = out_ref.shape[1] // size
        for k in range(blocks):
            cols = pl.ds(k * size, size)
            slot = where_ref[level, kind, d * blocks + k]

            @pl.when(slot >= 0)
            def _():
                out_ref[:, cols] = held[jnp.maximum(slot, 0)]

            @pl.when(slot < 0)
            def _():
                out_ref[:, cols] = jnp.zeros((size, size), out_ref.dtype)


def build_tables(level, where, count, tiles):
    slots, size = tiles.shape[3:5]
    out = jax.ShapeDtypeStruct((size, slots // 2 * size), tiles.dtype)
    outs = pl.pallas_call(
        lambda *refs: table_kernel(level, *refs),
        out_shape=[out] * 4,
        in_specs=[
            pl.BlockSpec(memory_space=pltpu.SMEM),
            pl.BlockSpec(memory_space=pltpu.SMEM),
            pl.BlockSpec(memory_space=pl.ANY),
        ],
        out_specs=[pl.BlockSpec(memory_space=pltpu.VMEM)] * 4,
        scratch_shapes=[pltpu.VMEM(tiles.shape[3:], tiles.dtype), pltpu.SemaphoreType.DMA],
        compiler_params=pltpu.CompilerParams(vmem_limit_bytes=VM << 20),
        cost_estimate=pl.CostEstimate(flops=0, bytes_accessed=12 << 20, transcendentals=0),
    )(where, count, tiles)
    return {"y": outs[:2], "z": outs[2:]}


def diagonal_solve(factor, values):
    return jnp.dot(
        factor, values, precision=lax.Precision.HIGH, preferred_element_type=jnp.float32
    )


def make_body(shape):
    orders = [gather_order(first, shape) for first in ("y", "z")]

    def body(rhs, tile_pairs, tiles, dinv):
        levels = rhs.shape[0]
        rhs, dinv, pairs = rhs[:, 0, 0], dinv[:, 0, 0], tile_pairs[:, 0, 0]
        me = lax.axis_index("grid") * shape[1] + lax.axis_index("proc")
        held = jnp.stack([jnp.asarray(order)[me] for order in orders])
        wanted = jnp.concatenate([held, held + shape[1]], 1)
        hit = pairs[:, None, None, :] == wanted[None, :, :, None]
        index = lax.broadcasted_iota(jnp.int32, hit.shape, 3)
        where = jnp.max(jnp.where(hit, index, -1), -1)
        counts = jnp.sum((pairs >= 0).astype(jnp.int32), 1)
        tables = [build_tables(t, where, counts, tiles) for t in range(levels - 1)]
        solved = [[None] * len(CHUNKS) for _ in range(levels)]
        sent = [None] * len(CHUNKS)
        for c, (first, start, width) in enumerate(CHUNKS):
            now = diagonal_solve(dinv[0], rhs[0, :, start : start + width])
            solved[0][c], sent[c] = lax.optimization_barrier((now, now.astype(jnp.bfloat16)))
        for level in range(1, levels):
            kind = LINK if level == levels - 1 else jnp.float32
            for c, (first, start, width) in enumerate(CHUNKS):
                here, there = tables[level - 1][first]
                blocks = gather_blocks(sent[c], first, shape)
                away = jnp.dot(there, blocks, preferred_element_type=jnp.float32)
                away = from_partner(away.astype(kind), shape, level - 1)
                stay = jnp.dot(here, blocks, preferred_element_type=jnp.float32)
                stay = lax.optimization_barrier(
                    rhs[level, :, start : start + width] - stay
                )
                now = diagonal_solve(dinv[level], stay - away.astype(jnp.float32))
                if level < levels - 1:
                    now = lax.optimization_barrier((now, now.astype(jnp.bfloat16)))
                    solved[level][c], sent[c] = now
                else:
                    solved[level][c] = lax.optimization_barrier(now)
        out = jnp.stack([jnp.concatenate(row, 1) for row in solved])[:, None, None]
        return out

    return body


def solution(mesh):
    shape = (mesh.shape["grid"], mesh.shape["proc"])
    return jax.shard_map(
        make_body(shape),
        mesh=mesh,
        in_specs=(
            P(None, "grid", "proc", None, None),
            P(None, "grid", "proc", None),
            P(None, "grid", "proc", None, None, None),
            P(None, "grid", "proc", None, None),
        ),
        out_specs=P(None, "grid", "proc", None, None),
        check_vma=False,
    )
```

```python
import jax
import jax.numpy as jnp
import numpy as np
from jax import lax
from jax.experimental import pallas as pl
from jax.experimental.pallas import tpu as pltpu
from jax.sharding import PartitionSpec as P

AXES = ("grid", "proc")
SIDE = 4
VM = 13
LINK = jnp.bfloat16
CHUNKS = (("y", 0, 256), ("z", 256, 256), ("y", 512, 256), ("z", 768, 256))


def ring_partner(place, flip):
    odd = place % 2
    return (place + 1 - 2 * (odd ^ flip)) % SIDE


def exchange_route(shape, axis, step):
    grids, procs = shape
    route = []
    for g in range(grids):
        for p in range(procs):
            z, y = divmod(p, SIDE)
            flip = (g + step) % 2
            if axis == "y":
                y = ring_partner(y, flip)
            else:
                z = ring_partner(z, flip)
            route.append((g * procs + p, g * procs + z * SIDE + y))
    return route


def gather_order(first, shape):
    grids, procs = shape
    table = np.zeros((grids * procs, procs), np.int32)
    for g in range(grids):
        for p in range(procs):

            def seq(t, flip=g % 2):
                near, far = ring_partner(t, flip), ring_partner(t, 1 - flip)
                return [t, near, far, ring_partner(far, flip)]

            z, y = divmod(p, SIDE)
            zs, ys = seq(z), seq(y)
            if first == "y":
                held = [a * SIDE + b for a in zs for b in ys]
            else:
                held = [a * SIDE + b for b in ys for a in zs]
            table[g * procs + p] = held
    return table


def gather_blocks(block, first, shape):
    held, got = block[None], None
    for axis in (first, "z" if first == "y" else "y"):
        for step in (0, 1):
            if got is not None:
                held = lax.optimization_barrier(jnp.concatenate([held, got]))
            got = lax.ppermute(held, AXES, exchange_route(shape, axis, step))
    return [blocks.reshape(-1, blocks.shape[-1]) for blocks in (held, got)]


def from_partner(block, shape, level):
    grids, procs = shape
    apart = 1 << level
    route = [(g * procs + p, (g ^ apart) * procs + p) for g in range(grids) for p in range(procs)]
    return lax.ppermute(block, AXES, route)


def table_kernel(level, where_ref, count_ref, tiles_ref, *refs):
    *out_refs, held, sem = refs
    count = count_ref[level]

    def copy(s):
        return pltpu.make_async_copy(tiles_ref.at[level, 0, 0, s], held.at[s], sem)

    def start(s, c):
        copy(s).start()
        return c

    def wait(s, c):
        copy(s).wait()
        return c

    lax.fori_loop(0, count, start, 0)
    lax.fori_loop(0, count, wait, 0)
    size = held.shape[1]
    for kind in range(len(out_refs) // 3):
        own_ref, here_ref, there_ref = out_refs[3 * kind : 3 * kind + 3]
        half = own_ref.shape[1] // size
        for k in range(2 * half):
            for d, got_ref in enumerate((here_ref, there_ref)):
                if k < half:
                    part = own_ref.at[pl.ds(d * size, size), pl.ds(k * size, size)]
                else:
                    part = got_ref.at[:, pl.ds((k - half) * size, size)]
                slot = where_ref[level, kind, d * 2 * half + k]

                @pl.when(slot >= 0)
                def _():
                    part[...] = held[jnp.maximum(slot, 0)]

                @pl.when(slot < 0)
                def _():
                    part[...] = jnp.zeros((size, size), part.dtype)


def build_tables(level, where, count, tiles):
    slots, size = tiles.shape[3:5]
    rows = (2 * size, size, size)
    out = [jax.ShapeDtypeStruct((n, slots // 4 * size), tiles.dtype) for n in rows * 2]
    outs = pl.pallas_call(
        lambda *refs: table_kernel(level, *refs),
        out_shape=out,
        in_specs=[
            pl.BlockSpec(memory_space=pltpu.SMEM),
            pl.BlockSpec(memory_space=pltpu.SMEM),
            pl.BlockSpec(memory_space=pltpu.HBM),
        ],
        out_specs=[pl.BlockSpec(memory_space=pltpu.VMEM)] * 6,
        scratch_shapes=[pltpu.VMEM(tiles.shape[3:], tiles.dtype), pltpu.SemaphoreType.DMA],
        compiler_params=pltpu.CompilerParams(vmem_limit_bytes=VM << 20),
        cost_estimate=pl.CostEstimate(flops=0, bytes_accessed=12 << 20, transcendentals=0),
    )(where, count, tiles)
    return {"y": outs[:3], "z": outs[3:]}


def diagonal_solve(factor, values):
    return jnp.dot(
        factor, values, precision=lax.Precision.HIGH, preferred_element_type=jnp.float32
    )


def make_body(shape):
    orders = [gather_order(first, shape) for first in ("y", "z")]

    def body(rhs, tile_pairs, tiles, dinv):
        levels, size = rhs.shape[0], rhs.shape[3]
        rhs, dinv, pairs = rhs[:, 0, 0], dinv[:, 0, 0], tile_pairs[:, 0, 0]
        me = lax.axis_index("grid") * shape[1] + lax.axis_index("proc")
        held = jnp.stack([jnp.asarray(order)[me] for order in orders])
        wanted = jnp.concatenate([held, held + shape[1]], 1)
        hit = pairs[:, None, None, :] == wanted[None, :, :, None]
        index = lax.broadcasted_iota(jnp.int32, hit.shape, 3)
        where = jnp.max(jnp.where(hit, index, -1), -1)
        counts = jnp.sum((pairs >= 0).astype(jnp.int32), 1)
        tiles = pltpu.with_memory_space_constraint(tiles, pltpu.HBM)
        tables = [build_tables(t, where, counts, tiles) for t in range(levels - 1)]
        solved = [[None] * len(CHUNKS) for _ in range(levels)]
        sent = [None] * len(CHUNKS)
        for c, (first, start, width) in enumerate(CHUNKS):
            now = diagonal_solve(dinv[0], rhs[0, :, start : start + width])
            solved[0][c], sent[c] = lax.optimization_barrier((now, now.astype(jnp.bfloat16)))
        for level in range(1, levels):
            kind = LINK if level == levels - 1 else jnp.float32
            for c, (first, start, width) in enumerate(CHUNKS):
                own, here, there = tables[level - 1][first]
                held, got = gather_blocks(sent[c], first, shape)
                part = jnp.dot(own, held, preferred_element_type=jnp.float32)
                part = lax.optimization_barrier(part)
                away = jnp.dot(there, got, preferred_element_type=jnp.float32)
                away = (away + part[size:]).astype(kind)
                away = from_partner(away, shape, level - 1)
                stay = jnp.dot(here, got, preferred_element_type=jnp.float32) + part[:size]
                stay = lax.optimization_barrier(
                    rhs[level, :, start : start + width] - stay
                )
                now = diagonal_solve(dinv[level], stay - away.astype(jnp.float32))
                if level < levels - 1:
                    now = lax.optimization_barrier((now, now.astype(jnp.bfloat16)))
                    solved[level][c], sent[c] = now
                else:
                    solved[level][c] = lax.optimization_barrier(now)
        solved[0] = lax.optimization_barrier((solved[0], sent))[0]
        out = jnp.stack([jnp.concatenate(row, 1) for row in solved])[:, None, None]
        return out

    return body


def solution(mesh):
    shape = (mesh.shape["grid"], mesh.shape["proc"])
    return jax.shard_map(
        make_body(shape),
        mesh=mesh,
        in_specs=(
            P(None, "grid", "proc", None, None),
            P(None, "grid", "proc", None),
            P(None, "grid", "proc", None, None, None),
            P(None, "grid", "proc", None, None),
        ),
        out_specs=P(None, "grid", "proc", None, None),
        check_vma=False,
    )
```
